32 devices in a mesh: region: 4 (over z), seq: 8 (over y, x, core).
Axes of the slice: x: 2, y: 2, z: 4, core: 2. Of those that a mesh axis runs over, the one named last changes fastest.
Arguments:
- queries: bfloat16 [4096, 1024], P(('region', 'seq')), may hold values from -80 to 80
- keys: bfloat16 [4096, 1024], P(('region', 'seq')), may hold values from -8 to 8
- values: bfloat16 [4096, 1024], P(('region', 'seq')), may hold values from -6 to 6
- out_grad: bfloat16 [4096, 1024], P(('region', 'seq')), may hold values from -6 to 6
- table: int32 [4, 8, 8], P('region'), may hold values from -1 to 23, as said below
- counts: int32 [4, 8], replicated, may hold values from 2 to 128
- sendlist: int32 [4, 2, 8], replicated, may hold values from 0 to 7, as said below
Outputs:
- attended: bfloat16 [4096, 1024], P(('region', 'seq'))
- query_grad: bfloat16 [4096, 1024], P(('region', 'seq'))
- key_grad: bfloat16 [4096, 1024], P(('region', 'seq'))
- value_grad: bfloat16 [4096, 1024], P(('region', 'seq'))
The draws below stay inside these ranges and needn't reach their ends.
Inputs may be any that keep to these rules, and one draw needn't show every extreme that they name: `table`: entry 0 of a block is the block itself; entries of one block differ; -1 marks padding and only follows live entries; an entry of 8 or more names boundary slot entry - 8 of key_ext. `sendlist`: the 8 blocks of one list differ.
All inputs are finite; a program needn't handle non-finite values.
Results may differ from the reference program's by a relative error of at most 0.035.
Values may be sent and summed in bfloat16 or wider, within the bound.
A program may use at most 128 MiB of HBM per device.

```python
import math
from functools import partial
import jax
import jax.numpy as jnp
from jax import lax

H = 16
HD = 64
D = 1024
BLK = 128
NBR = 8
BND = 8
REGIONS = 4
GAL_REG = 1024
NB = 8


def paired_draw(key):
    key_query, key_key = jax.random.split(jax.random.fold_in(key, 11), 2)
    total_rows = REGIONS * GAL_REG
    key_feats = jnp.clip(jax.random.normal(key_key, (total_rows, D), jnp.float32), -6.0, 6.0)
    query_feats = jnp.clip(jax.random.normal(key_query, (total_rows, D), jnp.float32), -6.0, 6.0)
    return (query_feats, key_feats)


def draw_queries(key, part):
    return paired_draw(key)[0].astype(jnp.bfloat16)


def draw_keys(key, part):
    return paired_draw(key)[1].astype(jnp.bfloat16)


def draw_table(key, part):
    key_live, key_step = jax.random.split(jax.random.fold_in(key, 23), 2)
    blocks = jnp.arange(NB, dtype=jnp.int32)
    live = jax.random.randint(key_live, (REGIONS, NB), 3, NBR + 1)
    live = jnp.where((blocks % 3 == 0)[None, :], NBR, live)
    stride = jax.random.randint(key_step, (REGIONS, NB), 1, 4)
    entry_ids = jnp.arange(NBR, dtype=jnp.int32)
    entries = (blocks[None, :, None] + entry_ids[None, None, :] * stride[:, :, None]) % (NB + 2 * BND)
    entries = jnp.where((blocks[None, :, None] == 0) & (entry_ids[None, None, :] == 1), NB + 2 * BND - 1, entries)
    return jnp.where(entry_ids[None, None, :] < live[:, :, None], entries, -1).astype(jnp.int32)


def draw_counts(key, part):
    drawn = jax.random.randint(jax.random.fold_in(key, 37), (REGIONS, NB), max(2, BLK // 8), BLK + 1)
    blocks = jnp.arange(NB, dtype=jnp.int32)
    return jnp.where((blocks % 5 == 0)[None, :], BLK, drawn).astype(jnp.int32)


def draw_sendlist(key, part):
    region_keys = jax.random.split(jax.random.fold_in(key, 41), REGIONS * 2)
    shuffled = jax.vmap(lambda one: jax.random.permutation(one, NB - 1))(region_keys).astype(jnp.int32)
    shuffled = shuffled.reshape(REGIONS, 2, NB - 1)[:, :, :BND - 1]
    prev_list = jnp.concatenate([jnp.zeros((REGIONS, 1), jnp.int32), shuffled[:, 0] + 1], axis=1)
    next_list = jnp.concatenate([jnp.full((REGIONS, 1), NB - 1, jnp.int32), shuffled[:, 1]], axis=1)
    return jnp.stack([prev_list, next_list], axis=1).astype(jnp.int32)


def steps_of(stream_key, extent, shards, low, largest):
    gain = 1.0
    for position, parts in shards:
        steps = jax.random.uniform(jax.random.fold_in(jax.random.fold_in(stream_key, 6), position), (parts,), jnp.float32, low / len(shards), largest / len(shards))
        gain = gain * jnp.repeat(jnp.exp(steps), extent[position] // parts).reshape((-1,) + (1,) * (len(extent) - 1 - position))
    return gain


def gaussian(key, dims, width, bound, cuts=(), held_as=jnp.bfloat16):
    gain = steps_of(key, dims, cuts, -0.22, 0.18) if cuts else 1.0
    values = jax.random.normal(key, dims, jnp.float32) * width * gain
    return jnp.minimum(jnp.maximum(values, -bound), bound).astype(held_as)


def setup_inputs(seed: int = 0) -> dict:
    seeds = jax.random.split(jax.random.key(seed), 8)
    queries = draw_queries(jax.random.fold_in(seeds[7], 71), 0)
    keys = draw_keys(jax.random.fold_in(seeds[7], 71), 0)
    values = gaussian(seeds[2], (REGIONS * GAL_REG, D), 1.0, 6.0, ((0, 32),))
    out_grad = gaussian(seeds[3], (REGIONS * GAL_REG, D), 1.0, 6.0, ((0, 32),))
    table = draw_table(jax.random.fold_in(seeds[7], 71), 0)
    counts = draw_counts(jax.random.fold_in(seeds[7], 71), 0)
    sendlist = draw_sendlist(jax.random.fold_in(seeds[7], 71), 0)
    return {"queries": queries, "keys": keys, "values": values, "out_grad": out_grad, "table": table, "counts": counts, "sendlist": sendlist}


def attend_group(carry, inputs, key_ext, value_ext, count_ext, scale):
    key_acc, value_acc = carry
    query_grp, grad_grp, table_grp, count_grp = inputs
    group_size, neighbours = table_grp.shape
    block_len = query_grp.shape[1]
    heads = query_grp.shape[2]
    depth = query_grp.shape[3]
    safe_ids = jnp.maximum(table_grp, 0).astype(jnp.int32)
    key_rows = key_ext[safe_ids].reshape(group_size, neighbours * block_len, heads, depth)
    value_rows = value_ext[safe_ids].reshape(group_size, neighbours * block_len, heads, depth)
    positions = jnp.arange(block_len, dtype=jnp.int32)
    key_valid = (table_grp >= 0)[:, :, None] & (positions[None, None, :] < count_ext[safe_ids][:, :, None])
    key_valid = key_valid.reshape(group_size, neighbours * block_len)
    query_valid = positions[None, :] < count_grp[:, None]
    highest = lax.Precision.HIGHEST
    scores = jnp.einsum('bqhe,bkhe->bhqk', query_grp.astype(jnp.float32), key_rows.astype(jnp.float32), precision=highest) * scale
    scores = jnp.where(key_valid[:, None, None, :], scores, jnp.float32(-1e+30))
    peak = lax.optimization_barrier(jnp.max(scores, axis=-1, keepdims=True))
    expo = jnp.exp(scores - peak)
    prob = (expo / lax.optimization_barrier(jnp.sum(expo, axis=-1, keepdims=True))).astype(jnp.bfloat16)
    prob_wide = prob.astype(jnp.float32)
    attended = jnp.einsum('bhqk,bkhe->bqhe', prob_wide, value_rows.astype(jnp.float32), precision=highest)
    attended = jnp.where(query_valid[:, :, None, None], attended, jnp.float32(0.0)).astype(jnp.bfloat16)
    grad_masked = jnp.where(query_valid[:, :, None, None], grad_grp, jnp.zeros_like(grad_grp))
    grad_wide = grad_masked.astype(jnp.float32)
    dprob = jnp.einsum('bqhe,bkhe->bhqk', grad_wide, value_rows.astype(jnp.float32), precision=highest)
    delta = lax.optimization_barrier(jnp.sum(grad_wide * attended.astype(jnp.float32), axis=-1))
    delta = jnp.transpose(delta, (0, 2, 1))[..., None]
    dscore = (prob_wide * (dprob - delta)).astype(jnp.bfloat16).astype(jnp.float32)
    query_grad = jnp.einsum('bhqk,bkhe->bqhe', dscore, key_rows.astype(jnp.float32), precision=highest) * scale
    query_grad = query_grad.astype(jnp.bfloat16)
    key_part = jnp.einsum('bhqk,bqhe->bkhe', dscore, query_grp.astype(jnp.float32), precision=highest) * scale
    value_part = jnp.einsum('bhqk,bqhe->bkhe', prob_wide, grad_wide, precision=highest)
    flat_ids = safe_ids.reshape(-1)
    key_acc = key_acc.at[flat_ids].add(key_part.reshape(group_size * neighbours, block_len, heads, depth))
    value_acc = value_acc.at[flat_ids].add(value_part.reshape(group_size * neighbours, block_len, heads, depth))
    return ((key_acc, value_acc), (attended, query_grad))

def reference(queries, keys, values, out_grad, table, counts, sendlist):
    shape_five = (REGIONS, NB, BLK, H, HD)
    query_blocks = queries.reshape(shape_five)
    key_blocks = keys.reshape(shape_five)
    value_blocks = values.reshape(shape_five)
    grad_blocks = out_grad.reshape(shape_five)
    choose = jax.vmap(lambda blocks, ids: blocks[ids])
    next_ids = sendlist[:, 1].astype(jnp.int32)
    prev_ids = sendlist[:, 0].astype(jnp.int32)
    key_ext = jnp.concatenate([key_blocks, jnp.roll(choose(key_blocks, next_ids), 1, axis=0), jnp.roll(choose(key_blocks, prev_ids), -1, axis=0)], axis=1)
    value_ext = jnp.concatenate([value_blocks, jnp.roll(choose(value_blocks, next_ids), 1, axis=0), jnp.roll(choose(value_blocks, prev_ids), -1, axis=0)], axis=1)
    count_ext = jnp.concatenate([counts, jnp.roll(choose(counts, next_ids), 1, axis=0), jnp.roll(choose(counts, prev_ids), -1, axis=0)], axis=1)
    scale = 1.0 / math.sqrt(HD)
    groups = NB // 4
    slots = NB + 2 * BND

    def one_region(items):
        query_reg, grad_reg, table_reg, count_reg, key_reg, value_reg, cext_reg = items
        start = (jnp.zeros((slots, BLK, H, HD), jnp.float32), jnp.zeros((slots, BLK, H, HD), jnp.float32))
        stepper = partial(attend_group, key_ext=key_reg, value_ext=value_reg, count_ext=cext_reg, scale=scale)
        carried, outputs = lax.scan(stepper, start, (query_reg.reshape(groups, 4, BLK, H, HD), grad_reg.reshape(groups, 4, BLK, H, HD), table_reg.reshape(groups, 4, NBR), count_reg.reshape(groups, 4)))
        return (outputs[0].reshape(NB, BLK, H, HD), outputs[1].reshape(NB, BLK, H, HD), carried[0], carried[1])
    attended, query_grad, key_acc, value_acc = lax.map(one_region, (query_blocks, grad_blocks, table, counts, key_ext, value_ext, count_ext))
    add_rows = jax.vmap(lambda own, ids, extra: own.at[ids].add(extra))

    def settle(accum):
        own = accum[:, :NB]
        own = add_rows(own, next_ids, jnp.roll(accum[:, NB:NB + BND], -1, axis=0))
        own = add_rows(own, prev_ids, jnp.roll(accum[:, NB + BND:], 1, axis=0))
        return own.reshape(REGIONS * GAL_REG, D).astype(jnp.bfloat16)
    return (attended.reshape(REGIONS * GAL_REG, D), query_grad.reshape(REGIONS * GAL_REG, D), settle(key_acc), settle(value_acc))
```

```python
from functools import partial
import math

import jax
import jax.numpy as jnp
from jax import lax
from jax.experimental import pallas as pl
from jax.experimental.pallas import tpu as pltpu
from jax.sharding import PartitionSpec as P

H = 16
HD = 64
BLK = 128
NBR = 8
BND = 8


def with_halo(cells, sides, width):
    for axis, dim in sides:
        count = lax.axis_size(axis)
        head = lax.slice_in_dim(cells, 0, width, axis=dim)
        tail = lax.slice_in_dim(cells, cells.shape[dim] - width, cells.shape[dim], axis=dim)
        cells = jnp.concatenate(
            [
                lax.ppermute(tail, axis, [(i, (i + 1) % count) for i in range(count)]),
                cells,
                lax.ppermute(head, axis, [((i + 1) % count, i) for i in range(count)]),
            ],
            axis=dim,
        )
    return cells


def attend_group(carry, inputs, key_ext, value_ext, count_ext, scale):
    key_acc, value_acc = carry
    query_grp, grad_grp, table_grp, count_grp, offset_grp = inputs
    group_size, neighbours = table_grp.shape
    heads = query_grp.shape[1]
    piece_len = query_grp.shape[2]
    depth = query_grp.shape[3]
    block_len = key_ext.shape[2]
    safe_ids = jnp.maximum(table_grp, 0)
    key_rows = key_ext[:, safe_ids].reshape(heads, group_size, neighbours * block_len, depth)
    value_rows = value_ext[:, safe_ids].reshape(heads, group_size, neighbours * block_len, depth)
    positions = jnp.arange(block_len, dtype=jnp.int32)
    key_valid = (table_grp >= 0)[:, :, None] & (
        positions[None, None, :] < count_ext[safe_ids][:, :, None]
    )
    key_valid = key_valid.reshape(group_size, neighbours * block_len)
    query_pos = jnp.arange(piece_len, dtype=jnp.int32)
    query_valid = offset_grp[:, None] + query_pos[None, :] < count_grp[:, None]
    scores = (
        jnp.einsum("bhqe,hbke->bhqk", query_grp, key_rows, preferred_element_type=jnp.float32)
        * scale
    )
    scores = jnp.where(key_valid[:, None, None, :], scores, jnp.float32(-1e30))
    peak = jnp.max(scores, axis=-1, keepdims=True)
    expo = jnp.exp(scores - peak)
    prob = (expo / jnp.sum(expo, axis=-1, keepdims=True)).astype(jnp.bfloat16)
    attended = jnp.einsum("bhqk,hbke->bhqe", prob, value_rows, preferred_element_type=jnp.float32)
    attended = jnp.where(query_valid[:, None, :, None], attended, jnp.float32(0.0)).astype(
        jnp.bfloat16
    )
    grad_masked = jnp.where(query_valid[:, None, :, None], grad_grp, jnp.zeros_like(grad_grp))
    dprob = jnp.einsum(
        "bhqe,hbke->bhqk", grad_masked, value_rows, preferred_element_type=jnp.float32
    )
    delta = jnp.sum(grad_masked.astype(jnp.float32) * attended.astype(jnp.float32), axis=-1)[
        ..., None
    ]
    dscore = (prob.astype(jnp.float32) * (dprob - delta)).astype(jnp.bfloat16)
    query_grad = (
        jnp.einsum("bhqk,hbke->bhqe", dscore, key_rows, preferred_element_type=jnp.float32) * scale
    )
    query_grad = query_grad.astype(jnp.bfloat16)
    key_part = (
        jnp.einsum("bhqk,bhqe->hbke", dscore, query_grp, preferred_element_type=jnp.float32) * scale
    )
    value_part = jnp.einsum(
        "bhqk,bhqe->hbke", prob, grad_masked, preferred_element_type=jnp.float32
    )
    flat_ids = safe_ids.reshape(-1)
    key_acc = key_acc.at[:, flat_ids].add(
        key_part.reshape(heads, group_size * neighbours, block_len, depth)
    )
    value_acc = value_acc.at[:, flat_ids].add(
        value_part.reshape(heads, group_size * neighbours, block_len, depth)
    )
    return ((key_acc, value_acc), (attended, query_grad))


def paired_body(queries, keys, values, out_grad, table, counts, sendlist):
    seq_count = lax.axis_size("seq")
    region_count = lax.axis_size("region")
    galaxies, width = queries.shape
    pair_count = seq_count // 2
    pair_heads = 2 * H // seq_count
    pair_width = pair_heads * HD
    half_rows = galaxies // 2
    region_rows = seq_count * galaxies
    block_total = region_rows // BLK
    parity = lax.axis_index("seq") % 2
    region_now = lax.axis_index("region")

    def half_slots(matrix):
        return (
            matrix.reshape(2, half_rows, pair_count, pair_width)
            .transpose(2, 0, 1, 3)
            .reshape(seq_count, half_rows, pair_width)
        )

    query_heads, grad_heads = (
        lax.all_to_all(half_slots(queries), "seq", split_axis=0, concat_axis=1, tiled=True),
        lax.all_to_all(half_slots(out_grad), "seq", split_axis=0, concat_axis=1, tiled=True),
    )

    def all_slots(matrix):
        grouped = matrix.reshape(galaxies, pair_count, pair_width).transpose(1, 0, 2)
        return jnp.repeat(grouped, 2, axis=0)

    key_heads, value_heads = (
        lax.all_to_all(all_slots(keys), "seq", split_axis=0, concat_axis=1, tiled=True),
        lax.all_to_all(all_slots(values), "seq", split_axis=0, concat_axis=1, tiled=True),
    )
    paired = jnp.stack([key_heads[0], value_heads[0]])
    head_first = paired.reshape(2, region_rows, pair_heads, HD).transpose(0, 2, 1, 3)
    head_blocks = head_first.reshape(2, pair_heads, block_total, BLK, HD)
    my_lists = sendlist[region_now]
    prev_ids = my_lists[0]
    next_ids = my_lists[1]
    rim_rows = BND * BLK
    packed_rim = rim_rows // 2
    outgoing = jnp.concatenate(
        [head_blocks[:, :, prev_ids], head_blocks[:, :, next_ids]], axis=2
    ).reshape(2, pair_heads, rim_rows, 2 * HD)
    widened = with_halo(outgoing, (("region", 2),), packed_rim)
    from_left = widened[:, :, :packed_rim].reshape(2, pair_heads, rim_rows, HD)
    from_right = widened[:, :, -packed_rim:].reshape(2, pair_heads, rim_rows, HD)
    slots = block_total + 2 * BND
    extended = jnp.concatenate([head_first, from_left, from_right], axis=2).reshape(
        2, pair_heads, slots, BLK, HD
    )
    left_region = (region_now + region_count - 1) % region_count
    right_region = (region_now + 1) % region_count
    count_ext = jnp.concatenate(
        [
            counts[region_now],
            counts[left_region][sendlist[left_region, 1]],
            counts[right_region][sendlist[right_region, 0]],
        ]
    )
    piece_rows = min(BLK, half_rows)
    per_source = half_rows // piece_rows
    piece_starts = (
        jnp.arange(seq_count, dtype=jnp.int32)[:, None] * galaxies
        + parity * half_rows
        + jnp.arange(per_source, dtype=jnp.int32)[None, :] * piece_rows
    ).reshape(-1)
    piece_blocks = piece_starts // BLK
    piece_offsets = piece_starts % BLK
    my_table = table[0][piece_blocks]
    my_counts = counts[region_now][piece_blocks]
    piece_total = seq_count * per_source
    group_width = 8
    groups = piece_total // group_width

    def scan_layout(matrix):
        return matrix.reshape(groups, group_width, piece_rows, pair_heads, HD).transpose(
            0, 1, 3, 2, 4
        )

    stepper = partial(
        attend_group,
        key_ext=extended[0],
        value_ext=extended[1],
        count_ext=count_ext,
        scale=1.0 / math.sqrt(HD),
    )
    start = (
        jnp.zeros((pair_heads, slots, BLK, HD), jnp.float32),
        jnp.zeros((pair_heads, slots, BLK, HD), jnp.float32),
    )
    carried, outputs = lax.scan(
        stepper,
        start,
        (
            scan_layout(query_heads),
            scan_layout(grad_heads),
            my_table.reshape(groups, group_width, NBR),
            my_counts.reshape(groups, group_width),
            piece_offsets.reshape(groups, group_width),
        ),
    )
    accum = jnp.stack([carried[0], carried[1]]).reshape(2, pair_heads, slots * BLK, HD)
    inner = accum[:, :, :region_rows].reshape(2, pair_heads, block_total, BLK, HD)
    rim_out = accum[:, :, region_rows:].reshape(2, pair_heads, rim_rows, 2 * HD)
    returned = with_halo(rim_out, (("region", 2),), packed_rim)
    back_left = returned[:, :, :packed_rim].reshape(2, pair_heads, BND, BLK, HD)
    back_right = returned[:, :, -packed_rim:].reshape(2, pair_heads, BND, BLK, HD)
    inner = inner.at[:, :, prev_ids].add(back_left)
    inner = inner.at[:, :, next_ids].add(back_right)
    inner = (
        inner.reshape(2, pair_heads, region_rows, HD)
        .transpose(0, 2, 1, 3)
        .reshape(2, region_rows, pair_width)
    )
    spread = lax.all_to_all(
        inner.reshape(2, seq_count, galaxies, pair_width),
        "seq",
        split_axis=1,
        concat_axis=1,
        tiled=True,
    )
    summed = spread.reshape(2, pair_count, 2, galaxies, pair_width).sum(axis=2)
    grads = summed.transpose(0, 2, 1, 3).reshape(2, galaxies, width)
    attended_heads = outputs[0].transpose(0, 1, 3, 2, 4).reshape(seq_count, half_rows, pair_width)
    qgrad_heads = outputs[1].transpose(0, 1, 3, 2, 4).reshape(seq_count, half_rows, pair_width)
    attended_back, qgrad_back = (
        lax.all_to_all(attended_heads, "seq", split_axis=0, concat_axis=0, tiled=True),
        lax.all_to_all(qgrad_heads, "seq", split_axis=0, concat_axis=0, tiled=True),
    )

    def owner_rows(received):
        return (
            received.reshape(pair_count, 2, half_rows, pair_width)
            .transpose(1, 2, 0, 3)
            .reshape(galaxies, width)
        )

    grads = grads.astype(jnp.bfloat16)
    return (owner_rows(attended_back), owner_rows(qgrad_back), grads[0], grads[1])


def attend_kernel(ids_ref, live_ref, counts_ref, q_ref, g_ref, own_ref, left_ref, right_ref,
                  att_ref, qg_ref, own_acc, left_out, right_out, ext, acc, *, blocks, heads):
    width = q_ref.shape[1]
    rows = blocks * BLK
    scale = 1.0 / math.sqrt(HD)
    for part in range(2):
        ext[part, :rows] = own_ref[part]
        ext[part, rows:2 * rows] = left_ref[part]
        ext[part, 2 * rows:] = right_ref[part]
    acc[...] = jnp.zeros_like(acc)
    lane_head = lax.broadcasted_iota(jnp.int32, (BLK, width), 1) // HD
    row_pos = lax.broadcasted_iota(jnp.int32, (BLK, width), 0)
    feat_head = lax.broadcasted_iota(jnp.int32, (width, BLK), 0) // HD
    query_lane = lax.broadcasted_iota(jnp.int32, (width, BLK), 1)
    key_pos = lax.broadcasted_iota(jnp.int32, (BLK, heads * BLK), 0)

    def stacked(block):
        return jnp.concatenate(
            [jnp.where(lane_head == h, block, 0.0) for h in range(heads)], axis=0
        ).astype(jnp.bfloat16)

    def unstacked(wide):
        out = wide[:, :BLK]
        for h in range(1, heads):
            out = jnp.where(feat_head == h, wide[:, h * BLK:(h + 1) * BLK], out)
        return out

    def one_block(b, carry):
        here = pl.ds(pl.multiple_of(b * BLK, BLK), BLK)
        count = counts_ref[b]
        slots = [
            pl.ds(pl.multiple_of(ids_ref[b * NBR + j] * BLK, BLK), BLK) for j in range(NBR)
        ]
        q_all = stacked(q_ref[here, :].astype(jnp.float32) * scale)
        grad = jnp.where(row_pos < count, g_ref[here, :].astype(jnp.float32), 0.0)
        g_all = stacked(grad)
        k = jnp.concatenate([ext[0, s, :] for s in slots], axis=0)
        v = jnp.concatenate([ext[1, s, :] for s in slots], axis=0)
        scores = lax.dot_general(
            k, q_all, (((1,), (1,)), ((), ())), preferred_element_type=jnp.float32
        )
        scores = jnp.concatenate(
            [
                jnp.where(
                    key_pos < live_ref[b * NBR + j],
                    scores[j * BLK:(j + 1) * BLK],
                    jnp.float32(-1e30),
                )
                for j in range(NBR)
            ],
            axis=0,
        )
        peak = jnp.max(scores, axis=0, keepdims=True)
        expo = jnp.exp(scores - peak)
        inverse = 1.0 / jnp.sum(expo, axis=0, keepdims=True)
        prob = (expo * inverse).astype(jnp.bfloat16)
        att_wide = lax.dot_general(
            v, prob, (((0,), (0,)), ((), ())), preferred_element_type=jnp.float32
        )
        att = unstacked(att_wide)
        att = jnp.where(query_lane < count, att, 0.0).astype(jnp.bfloat16).astype(jnp.float32)
        att_ref[here, :] = att.T.astype(jnp.bfloat16)
        prod = grad.T * att
        delta = jnp.concatenate(
            [
                jnp.sum(prod[h * HD:(h + 1) * HD], axis=0, keepdims=True)
                for h in range(heads)
            ],
            axis=1,
        )
        dprob = lax.dot_general(
            v, g_all, (((1,), (1,)), ((), ())), preferred_element_type=jnp.float32
        )
        dscore = (prob.astype(jnp.float32) * (dprob - delta)).astype(jnp.bfloat16)
        qg_wide = lax.dot_general(
            k, dscore, (((0,), (0,)), ((), ())), preferred_element_type=jnp.float32
        )
        qg_ref[here, :] = (unstacked(qg_wide).T * scale).astype(jnp.bfloat16)
        dk = jnp.dot(dscore, q_all, preferred_element_type=jnp.float32)
        dv = jnp.dot(prob, g_all, preferred_element_type=jnp.float32)
        for j in range(NBR):
            acc[0, slots[j], :] += dk[j * BLK:(j + 1) * BLK]
            acc[1, slots[j], :] += dv[j * BLK:(j + 1) * BLK]
        return carry

    lax.fori_loop(0, blocks, one_block, 0)
    for part in range(2):
        own_acc[part] = acc[part, :rows]
        left_out[part] = acc[part, rows:2 * rows].astype(jnp.bfloat16)
        right_out[part] = acc[part, 2 * rows:].astype(jnp.bfloat16)


def slab_ids(table, counts, sendlist, region_now, region_count, blocks):
    left = (region_now + region_count - 1) % region_count
    right = (region_now + 1) % region_count
    remap = jnp.concatenate(
        [
            jnp.arange(blocks, dtype=jnp.int32),
            blocks + sendlist[left, 1],
            2 * blocks + sendlist[right, 0],
        ]
    )
    slab_counts = jnp.concatenate([counts[region_now], counts[left], counts[right]])
    ids = remap[jnp.maximum(table[0], 0)]
    live = jnp.where(table[0] >= 0, slab_counts[ids], 0)
    return ids.reshape(-1), live.reshape(-1), counts[region_now]


def head_body(queries, keys, values, out_grad, table, counts, sendlist):
    seq_count = lax.axis_size("seq")
    region_count = lax.axis_size("region")
    galaxies, features = queries.shape
    width = features // seq_count
    heads = width // HD
    rows = seq_count * galaxies
    blocks = rows // BLK
    region_now = lax.axis_index("region")
    ids, live, my_counts = slab_ids(table, counts, sendlist, region_now, region_count, blocks)

    def to_heads(first, second):
        pair = jnp.stack([first, second]).reshape(2, galaxies, seq_count, width)
        sent = lax.all_to_all(
            pair.transpose(2, 0, 1, 3), "seq", split_axis=0, concat_axis=0, tiled=True
        )
        return sent.transpose(1, 0, 2, 3).reshape(2, rows, width)

    def to_rows(first, second):
        pair = jnp.stack([first, second]).reshape(2, seq_count, galaxies, width)
        sent = lax.all_to_all(
            pair.transpose(1, 0, 2, 3), "seq", split_axis=0, concat_axis=0, tiled=True
        )
        return sent.transpose(1, 2, 0, 3).reshape(2, galaxies, features)

    up = [(i, (i + 1) % region_count) for i in range(region_count)]
    down = [((i + 1) % region_count, i) for i in range(region_count)]
    own = to_heads(keys, values)
    left = lax.ppermute(own, "region", up)
    right = lax.ppermute(own, "region", down)
    query_grad_in = to_heads(queries, out_grad)
    vmem = pl.BlockSpec(memory_space=pltpu.VMEM)
    smem = pl.BlockSpec(memory_space=pltpu.SMEM)
    slab = jax.ShapeDtypeStruct((2, rows, width), jnp.bfloat16)
    flat = jax.ShapeDtypeStruct((rows, width), jnp.bfloat16)
    attended, query_grad, inner, to_left, to_right = pl.pallas_call(
        partial(attend_kernel, blocks=blocks, heads=heads),
        out_shape=(flat, flat, jax.ShapeDtypeStruct((2, rows, width), jnp.float32), slab, slab),
        in_specs=[smem] * 3 + [vmem] * 5,
        out_specs=[vmem] * 5,
        scratch_shapes=[
            pltpu.VMEM((2, 3 * rows, width), jnp.bfloat16),
            pltpu.VMEM((2, 3 * rows, width), jnp.float32),
        ],
        compiler_params=pltpu.CompilerParams(vmem_limit_bytes=40 * 1024 * 1024),
    )(ids, live, my_counts, query_grad_in[0], query_grad_in[1], own, left, right)
    from_right = lax.ppermute(to_left, "region", down)
    from_left = lax.ppermute(to_right, "region", up)
    front = to_rows(attended, query_grad)
    total = inner + from_right.astype(jnp.float32) + from_left.astype(jnp.float32)
    total = total.astype(jnp.bfloat16)
    grads = to_rows(total[0], total[1])
    return (front[0], front[1], grads[0], grads[1])


def solution(mesh):
    whole_heads = H % mesh.shape["seq"] == 0

    def body(queries, *rest):
        blocks = mesh.shape["seq"] * queries.shape[0] // BLK
        form = head_body if whole_heads and blocks == BND else paired_body
        return form(queries, *rest)

    return jax.shard_map(
        body,
        mesh=mesh,
        in_specs=(
            P(("region", "seq"), None),
            P(("region", "seq"), None),
            P(("region", "seq"), None),
            P(("region", "seq"), None),
            P("region", None, None),
            P(),
            P(),
        ),
        out_specs=(
            P(("region", "seq"), None),
            P(("region", "seq"), None),
            P(("region", "seq"), None),
            P(("region", "seq"), None),
        ),
        check_vma=False,
    )
```
